32 devices in a mesh: events: 2 (over y), blk: 4 (over z), sub: 2 (over x), pair: 2 (over core).
Axes of the slice: x: 2, y: 2, z: 4, core: 2. Of those that a mesh axis runs over, the one named last changes fastest.
Arguments:
- synthetic: bfloat16 [2560, 4096], P(('events', 'sub', 'pair'), 'blk'), parts along dimension 0, may hold values from -6 to 6
- observed: bfloat16 [2560, 4096], P(('events', 'sub', 'pair'), 'blk'), parts along dimension 0, may hold values from -6 to 6
- station_weights: int32 [2560], P('events'), parts along dimension 0, may hold values from 1 to 4
- pair_mask: int32 [32, 16], P('events'), parts along dimension 0, may hold values from 0 to 1, as said below
Outputs:
- adjoint_traces: bfloat16 [2560, 4096], P(('events', 'sub', 'pair'), 'blk'), parts along dimension 0
The draws below stay inside these ranges and needn't reach their ends.
There are 2 independent parts, one for each index of `events`. The reference program is written for one: setup_inputs(seed, part) draws one part's arguments, and reference() takes and returns one part's arrays. A program takes and returns all parts, laid end to end along the dimension named above; each array names one. Nothing has to cross between parts.
Inputs may be any that keep to these rules, and one draw needn't show every extreme that they name: pair_mask[p, q] is 1 where station pieces p and q are coupled; piece p holds stations p * 80 to (p + 1) * 80 - 1.
All inputs are finite; a program needn't handle non-finite values.
Results may differ from the reference program's by a relative error of at most 0.025.
Values may be sent and summed in bfloat16 or wider, within the bound.
A program may use at most 64 MiB of HBM per device.

```python
import math
import jax
import jax.numpy as jnp
from jax import lax

NT = 4096
NF = 512
F_LO = 64
PIECE = 80
CYCLE = 4
STATIONS = 1280
NPIECE = 16


def draw_pair_mask(key, part):
    level_key = jax.random.fold_in(key, 11)
    entry_key = jax.random.fold_in(key, 12)
    levels = jax.random.randint(level_key, (CYCLE,), 0, 5)
    entries = jax.random.randint(entry_key, (NPIECE, NPIECE), 0, 4)
    bands = jnp.arange(NPIECE, dtype=jnp.int32) % CYCLE
    piece_level = levels[bands]
    bound = jnp.minimum(piece_level[:, None], piece_level[None, :])
    return (entries < bound).astype(jnp.int32)


def touch_ends(drawn, rng, low, top_value):
    spot = [jax.random.randint(jax.random.fold_in(rng, axis), (), 0, length) for axis, length in enumerate(drawn.shape)]
    main_axis = drawn.shape.index(max(drawn.shape))
    neighbour = spot[:main_axis] + [(spot[main_axis] + 1) % drawn.shape[main_axis]] + spot[main_axis + 1:]
    return drawn.at[tuple(spot)].set(low).at[tuple(neighbour)].set(top_value)


def shard_levels(rng, extent, pieces, smallest, high):
    def one(dim, blocks):
        heights = jax.random.uniform(jax.random.fold_in(jax.random.fold_in(rng, 6), dim), (blocks,), jnp.float32, smallest / len(pieces), high / len(pieces))
        return jnp.repeat(jnp.exp(heights), extent[dim] // blocks).reshape((-1,) + (1,) * (len(extent) - dim - 1))

    gain = one(*pieces[0])
    for cut in pieces[1:]:
        gain = gain * one(*cut)
    return gain


def noise(stream_key, shape, deviation, most, shards=(), kind=jnp.bfloat16):
    values = jax.random.normal(stream_key, shape, jnp.float32) * deviation
    if len(shards) > 0:
        values = shard_levels(stream_key, shape, shards, -0.22, 0.18) * values
    return jnp.clip(values, min=-most, max=most).astype(kind)


def setup_inputs(seed: int = 0, part: int = 0) -> dict:
    key_of = jax.random.split(jax.random.key(seed), 5)
    own_keys = jax.random.split(jax.random.fold_in(key_of[4], part), 5)
    return {
        "synthetic": noise(own_keys[0], (STATIONS, NT), 1.0, 6.0, ((0, 4), (1, 4))),
        "observed": noise(own_keys[1], (STATIONS, NT), 1.0, 6.0, ((0, 4), (1, 4))),
        "station_weights": touch_ends(jax.random.randint(own_keys[2], (STATIONS,), 1, 5), jax.random.fold_in(own_keys[2], 1), 1, 4).astype(jnp.int32),
        "pair_mask": draw_pair_mask(jax.random.fold_in(jax.random.fold_in(key_of[4], part), 71), part),
    }


epsilon = 1e-06

def make_basis(first_sample, sample_count):
    sample_index = first_sample + jnp.arange(sample_count, dtype=jnp.int32)
    bin_index = F_LO + jnp.arange(NF, dtype=jnp.int32)
    phases = sample_index[:, None] * bin_index[None, :] % NT
    angles = phases.astype(jnp.float32) * (2.0 * math.pi / NT)
    return jnp.concatenate([jnp.cos(angles), -jnp.sin(angles)], axis=1).astype(jnp.bfloat16)

def spectral_rate(spectrum):
    angular = 2.0 * math.pi / NT * (F_LO + jnp.arange(NF, dtype=jnp.int32)).astype(jnp.float32)
    widened = spectrum.astype(jnp.float32)
    return jnp.concatenate([-angular * widened[:, NF:], angular * widened[:, :NF]], axis=1).astype(jnp.bfloat16)

def reference(synthetic, observed, station_weights, pair_mask):
    basis = make_basis(0, NT)
    scale_factor = 1.0 / math.sqrt(NT)
    model_spec = (jnp.dot(synthetic, basis, preferred_element_type=jnp.float32) * scale_factor).astype(jnp.bfloat16)
    data_spec = (jnp.dot(observed, basis, preferred_element_type=jnp.float32) * scale_factor).astype(jnp.bfloat16)
    model_rate = spectral_rate(model_spec)
    data_rate = spectral_rate(data_spec)
    power = lax.optimization_barrier(jnp.sum(jnp.square(model_rate.astype(jnp.float32)), axis=1))
    link_piece = jnp.maximum(pair_mask, pair_mask.T)
    gains = station_weights.astype(jnp.float32)
    factor = 4.0 / math.sqrt(STATIONS)
    rows_per = math.gcd(STATIONS, 128)
    starts = jnp.arange(0, STATIONS, rows_per, dtype=jnp.int32)

    def one_block(row_start):
        row_ids = row_start + jnp.arange(rows_per, dtype=jnp.int32)
        model_rows = lax.dynamic_slice_in_dim(model_spec, row_start, rows_per, 0)
        data_rows = lax.dynamic_slice_in_dim(data_spec, row_start, rows_per, 0)
        cross_model = jnp.dot(model_rows, model_rate.T, preferred_element_type=jnp.float32)
        cross_data = jnp.dot(data_rows, data_rate.T, preferred_element_type=jnp.float32)
        link_rows = jnp.repeat(link_piece[row_ids // PIECE], PIECE, axis=1).astype(jnp.float32)
        row_power = lax.dynamic_slice_in_dim(power, row_start, rows_per, 0)
        row_gain = lax.dynamic_slice_in_dim(gains, row_start, rows_per, 0)
        normalizer = 0.5 * (row_power[:, None] + power[None, :]) + epsilon
        coupling = (factor * row_gain[:, None] * gains[None, :] * link_rows * (cross_model - cross_data) / normalizer).astype(jnp.bfloat16)
        return jnp.dot(coupling, model_rate, preferred_element_type=jnp.float32)
    adjoint_spec = lax.map(one_block, starts).reshape(STATIONS, 2 * NF).astype(jnp.bfloat16)
    inverse_scale = 1.0 / math.sqrt(NF)
    return (jnp.dot(adjoint_spec, basis.T, preferred_element_type=jnp.float32) * inverse_scale).astype(jnp.bfloat16)
```

```python
import functools
import math

import jax
import jax.numpy as jnp
from jax import lax
from jax.experimental import pallas as pl
from jax.experimental.pallas import tpu as pltpu
from jax.sharding import PartitionSpec as P

NT = 4096
NF = 512
F_LO = 64


epsilon = 1e-06


def from_behind(value, axis, steps):
    count = lax.axis_size(axis)
    pairs = [(source, (source + steps) % count) for source in range(count)]
    return lax.ppermute(value, axis, pairs)


def make_basis(first_sample, sample_count):
    sample_index = first_sample + jnp.arange(sample_count, dtype=jnp.int32)
    bin_index = F_LO + jnp.arange(NF, dtype=jnp.int32)
    phases = sample_index[:, None] * bin_index[None, :] % NT
    angles = phases.astype(jnp.float32) * (2.0 * math.pi / NT)
    return jnp.concatenate([jnp.cos(angles), -jnp.sin(angles)], axis=1).astype(jnp.bfloat16)


def spectral_rate(spectrum):
    angular = 2.0 * math.pi / NT * (F_LO + jnp.arange(NF, dtype=jnp.int32)).astype(jnp.float32)
    widened = spectrum.astype(jnp.float32)
    return jnp.concatenate([-angular * widened[:, NF:], angular * widened[:, :NF]], axis=1).astype(
        jnp.bfloat16
    )


def shards(synthetic, observed, station_weights, pair_mask):
    cycle_size = lax.axis_size("blk")
    groups = lax.axis_size("sub") * lax.axis_size("pair")
    block_index = lax.axis_index("blk")
    member = lax.axis_index("sub") * lax.axis_size("pair") + lax.axis_index("pair")
    time_span = synthetic.shape[1]
    piece_rows = synthetic.shape[0] // cycle_size
    stations = station_weights.shape[0]
    scale_factor = 1.0 / math.sqrt(NT)
    inverse_scale = 1.0 / math.sqrt(NF)
    contract_last = (((1,), (1,)), ((), ()))
    basis_rows = make_basis(block_index * time_span, time_span)
    summed = lax.psum_scatter(
        jnp.concatenate(
            [
                jnp.dot(synthetic, basis_rows, preferred_element_type=jnp.float32),
                jnp.dot(observed, basis_rows, preferred_element_type=jnp.float32),
            ],
            axis=1,
        ).astype(jnp.bfloat16),
        "blk",
        scatter_dimension=0,
        tiled=True,
    ).astype(jnp.float32)
    model_spec = (summed[:, : 2 * NF] * scale_factor).astype(jnp.bfloat16)
    data_spec = (summed[:, 2 * NF :] * scale_factor).astype(jnp.bfloat16)
    own_rates = jnp.concatenate([spectral_rate(model_spec), spectral_rate(data_spec)], axis=1)
    block_model, block_data = (
        lax.all_gather(model_spec, ("sub", "pair"), axis=0, tiled=True),
        lax.all_gather(data_spec, ("sub", "pair"), axis=0, tiled=True),
    )
    block_power = jnp.sum(jnp.square(spectral_rate(block_model).astype(jnp.float32)), axis=1)
    gains = station_weights.astype(jnp.float32).reshape(groups * cycle_size, piece_rows)
    block_gain = lax.dynamic_slice_in_dim(
        gains.reshape(groups, cycle_size, piece_rows), block_index, 1, 1
    ).reshape(groups * piece_rows)
    link_piece = jnp.maximum(pair_mask, pair_mask.T)
    block_link = lax.dynamic_slice_in_dim(
        link_piece.reshape(groups, cycle_size, groups * cycle_size), block_index, 1, 1
    ).reshape(groups, groups * cycle_size)
    factor = 4.0 / math.sqrt(stations)

    def pair_tile(running, carried, source):
        column_model = carried[:, : 2 * NF]
        column_data = carried[:, 2 * NF :]
        column_piece = member * cycle_size + source
        column_gain = lax.dynamic_slice_in_dim(gains, column_piece, 1, 0)[0]
        column_power = jnp.sum(jnp.square(column_model.astype(jnp.float32)), axis=1)
        active_flags = lax.dynamic_slice_in_dim(block_link, column_piece, 1, 1)[:, 0]
        link_rows = jnp.broadcast_to(
            active_flags.astype(jnp.float32)[:, None], (groups, piece_rows)
        ).reshape(groups * piece_rows)
        cross_model = lax.dot_general(
            block_model, column_model, contract_last, preferred_element_type=jnp.float32
        )
        cross_data = lax.dot_general(
            block_data, column_data, contract_last, preferred_element_type=jnp.float32
        )
        normalizer = 0.5 * (block_power[:, None] + column_power[None, :]) + epsilon
        coupling = (
            factor
            * block_gain[:, None]
            * column_gain[None, :]
            * link_rows[:, None]
            * (cross_model - cross_data)
            / normalizer
        ).astype(jnp.bfloat16)
        return running + jnp.dot(coupling, column_model, preferred_element_type=jnp.float32)

    running = jnp.zeros((groups * piece_rows, 2 * NF), jnp.float32)
    running = pair_tile(running, own_rates, block_index)

    def cycle_turn(turn_index, loop_state):
        current, ahead_rates, behind_rates = loop_state
        ahead_rates = from_behind(ahead_rates, "blk", 1)
        behind_rates = from_behind(behind_rates, "blk", -1)
        current = pair_tile(current, ahead_rates, (block_index - turn_index) % cycle_size)
        current = pair_tile(current, behind_rates, (block_index + turn_index) % cycle_size)
        return (current, ahead_rates, behind_rates)

    running, ahead_rates, behind_rates = lax.fori_loop(
        1, cycle_size // 2, cycle_turn, (running, own_rates, own_rates)
    )
    ahead_rates = from_behind(ahead_rates, "blk", 1)
    running = pair_tile(running, ahead_rates, (block_index - cycle_size // 2) % cycle_size)
    adjoint_spec = lax.psum_scatter(
        running.astype(jnp.bfloat16), ("sub", "pair"), scatter_dimension=0, tiled=True
    )
    return (
        lax.dot_general(
            lax.all_gather(adjoint_spec, "blk", axis=0, tiled=True),
            basis_rows,
            contract_last,
            preferred_element_type=jnp.float32,
        )
        * inverse_scale
    ).astype(jnp.bfloat16)


MESH = pl.DeviceIdType.MESH
RC = 32
FINE = 32
TILE = 256


def trig(samples, shape):
    bins = F_LO + lax.broadcasted_iota(jnp.int32, shape, 1)
    angle = ((samples * bins) % NT).astype(jnp.float32) * (2.0 * math.pi / NT)
    return jnp.cos(angle), jnp.sin(angle)


def fused_kernel(
    steps_z, factor, syn, obs, weights, mask, out,
    basis, tab, part, go_up, go_down, from_low, from_high, spec, own_rows, rates,
    power_col, power_row, gain, acc,
    send_z, recv_z, send_x, send_c, send_relay, recv_g,
):
    f32, bf16 = jnp.float32, jnp.bfloat16
    event, z = lax.axis_index("events"), lax.axis_index("blk")
    sub, core = lax.axis_index("sub"), lax.axis_index("pair")
    last = steps_z - 1
    rows, span = syn.shape
    stations = weights.shape[1]
    pieces = mask.shape[0]
    chunks = rows // RC
    me, across = sub * 2 + core, (1 - sub) * 2 + core
    twin, diagonal = sub * 2 + 1 - core, (1 - sub) * 2 + 1 - core
    up, down = (event, z + 1, sub, core), (event, z - 1, sub, core)
    over, beside = (event, z, 1 - sub, core), (event, z, sub, 1 - core)

    barrier = pltpu.get_barrier_semaphore()
    for device in (over, beside):
        pl.semaphore_signal(barrier, inc=1, device_id=device, device_id_type=MESH)

    @pl.when(z > 0)
    def _():
        pl.semaphore_signal(barrier, inc=1, device_id=down, device_id_type=MESH)

    @pl.when(z < last)
    def _():
        pl.semaphore_signal(barrier, inc=1, device_id=up, device_id_type=MESH)

    coarse = span // FINE
    shape = (coarse, NF)
    coarse_cos, coarse_sin = trig(
        z * span + FINE * lax.broadcasted_iota(jnp.int32, shape, 0), shape
    )
    tab[0] = coarse_cos
    tab[1] = coarse_sin
    shape = (FINE, NF)
    fine_cos, fine_sin = trig(lax.broadcasted_iota(jnp.int32, shape, 0), shape)

    def fill(a, carry):
        c = tab[0, pl.ds(a, 1), :]
        s = tab[1, pl.ds(a, 1), :]
        at = pl.ds(pl.multiple_of(a * FINE, FINE), FINE)
        basis[at, :NF] = (c * fine_cos - s * fine_sin).astype(bf16)
        basis[at, NF:] = (-(s * fine_cos + c * fine_sin)).astype(bf16)
        return carry

    lax.fori_loop(0, coarse, fill, 0)

    scale = 1.0 / math.sqrt(NT)

    def project(j, carry):
        at = pl.ds(pl.multiple_of(j * TILE, TILE), TILE)
        columns = basis[:, at]
        for k, traces in enumerate((syn, obs)):
            value = jnp.dot(traces[...], columns, preferred_element_type=f32) * scale
            part[:, k * RC : (k + 1) * RC, at] = value.astype(bf16).reshape(chunks, RC, TILE)
        return carry

    lax.fori_loop(0, 2 * NF // TILE, project, 0)

    peers = 2 + jnp.where(z > 0, 1, 0) + jnp.where(z < last, 1, 0)
    pl.semaphore_wait(barrier, peers)

    def remote(source, target, send, recv, device):
        return pltpu.make_async_remote_copy(
            src_ref=source, dst_ref=target, send_sem=send, recv_sem=recv,
            device_id=device, device_id_type=MESH,
        )

    def upward(source, n):
        return remote(source.at[n], from_low.at[n], send_z.at[0, n], recv_z.at[0, n], up)

    def downward(source, n):
        return remote(source.at[n], from_high.at[n], send_z.at[1, n], recv_z.at[1, n], down)

    def to_over(n):
        return remote(spec.at[me, n], spec.at[me, n], send_x.at[n], recv_g.at[me, n], over)

    def to_beside(n):
        return remote(spec.at[me, n], spec.at[me, n], send_c.at[n], recv_g.at[me, n], beside)

    def relay(n):
        return remote(
            spec.at[across, n], spec.at[across, n], send_relay.at[n], recv_g.at[across, n], beside
        )

    def arrived(member, n):
        remote(spec.at[member, n], spec.at[member, n], send_x.at[n], recv_g.at[member, n], over).wait_recv()

    @pl.when(z == 0)
    def _():
        lax.fori_loop(0, chunks, lambda n, c: (upward(part, n).start(), c)[1], 0)
        from_low[...] = jnp.zeros_like(from_low)

    @pl.when(z == last)
    def _():
        lax.fori_loop(0, chunks, lambda n, c: (downward(part, n).start(), c)[1], 0)
        from_high[...] = jnp.zeros_like(from_high)

    span_piece = stations // pieces
    own_station = me * rows + lax.broadcasted_iota(jnp.int32, (rows, pieces), 0)
    behind = own_station - span_piece * lax.broadcasted_iota(jnp.int32, (rows, pieces), 1)
    own_piece = jnp.where((behind >= 0) & (behind < span_piece), 1.0, 0.0).astype(bf16)
    links = mask[...].astype(f32).astype(bf16)
    link_there = jnp.dot(own_piece, links, preferred_element_type=f32).astype(bf16)
    link_back = lax.dot_general(
        own_piece, links, (((1,), (1,)), ((), ())), preferred_element_type=f32
    ).astype(bf16)
    station = lax.broadcasted_iota(jnp.int32, (pieces, stations), 1)
    behind = station - span_piece * lax.broadcasted_iota(jnp.int32, (pieces, stations), 0)
    every_piece = jnp.where((behind >= 0) & (behind < span_piece), 1.0, 0.0).astype(bf16)
    gain_row = weights[...].astype(f32)
    column = lax.broadcasted_iota(jnp.int32, (rows, stations), 1)
    row = me * rows + lax.broadcasted_iota(jnp.int32, (rows, stations), 0)
    gain_col = jnp.sum(jnp.where(column == row, gain_row, 0.0), axis=1, keepdims=True)
    gain[...] = (factor * gain_col) * gain_row * jnp.maximum(
        jnp.dot(link_there, every_piece, preferred_element_type=f32),
        jnp.dot(link_back, every_piece, preferred_element_type=f32),
    )

    angular = 2.0 * math.pi / NT * (
        F_LO + lax.broadcasted_iota(jnp.int32, (1, NF), 1)
    ).astype(f32)

    def take(member, n):
        at = pl.ds(pl.multiple_of(member * rows + n * RC, RC), RC)
        value = spec[member, n].astype(f32)
        model_lo = (-angular * value[:RC, NF:]).astype(bf16)
        model_hi = (angular * value[:RC, :NF]).astype(bf16)
        rates[at, :NF] = model_lo
        rates[at, NF : 2 * NF] = model_hi
        rates[at, 2 * NF : 3 * NF] = (angular * value[RC:, NF:]).astype(bf16)
        rates[at, 3 * NF :] = (-angular * value[RC:, :NF]).astype(bf16)
        square = jnp.square(model_lo.astype(f32)) + jnp.square(model_hi.astype(f32))
        power_col[at, :] = jnp.broadcast_to(
            jnp.sum(square, axis=1, keepdims=True), (RC, 128)
        )

    def within(n):
        return (n >= 0) & (n < chunks)

    far = jnp.maximum(z, last - z)

    def step(s, carry):
        n_low, n_high, n_own = s - z, s - (last - z), s - far

        @pl.when(within(n_low) & (z > 0))
        def _():
            upward(part, n_low).wait_recv()

            @pl.when(z < last)
            def _():
                go_up[n_low] = (part[n_low].astype(f32) + from_low[n_low].astype(f32)).astype(bf16)
                upward(go_up, n_low).start()

        @pl.when(within(n_high) & (z < last))
        def _():
            downward(part, n_high).wait_recv()

            @pl.when(z > 0)
            def _():
                go_down[n_high] = (
                    part[n_high].astype(f32) + from_high[n_high].astype(f32)
                ).astype(bf16)
                downward(go_down, n_high).start()

        @pl.when(within(n_own))
        def _():
            spec[me, n_own] = (
                part[n_own].astype(f32)
                + from_low[n_own].astype(f32)
                + from_high[n_own].astype(f32)
            ).astype(bf16)
            to_over(n_own).start()
            to_beside(n_own).start()
            at = pl.ds(pl.multiple_of(n_own * RC, RC), RC)
            own_rows[at, : 2 * NF] = spec[me, n_own, :RC, :]
            own_rows[at, 2 * NF :] = spec[me, n_own, RC:, :]
            take(me, n_own)

        @pl.when(within(n_own - 2))
        def _():
            n = n_own - 2
            arrived(across, n)
            relay(n).start()
            arrived(twin, n)
            take(across, n)
            take(twin, n)

        @pl.when(within(n_own - 3))
        def _():
            n = n_own - 3
            arrived(diagonal, n)
            take(diagonal, n)

        return carry

    lax.fori_loop(0, chunks + last + 3, step, 0)

    eye = lax.broadcasted_iota(jnp.int32, (128, 128), 0) == lax.broadcasted_iota(
        jnp.int32, (128, 128), 1
    )

    def turn(q, carry):
        at = pl.ds(pl.multiple_of(q * 128, 128), 128)
        power_row[:, at] = jnp.sum(
            jnp.where(eye, power_col[at, :], 0.0), axis=0, keepdims=True
        )
        return carry

    lax.fori_loop(0, stations // 128, turn, 0)
    own_power = power_col[pl.ds(pl.multiple_of(me * rows, RC), rows), :][:, :1]
    acc[...] = jnp.zeros_like(acc)

    def pair_tile(q, carry):
        at = pl.ds(pl.multiple_of(q * TILE, TILE), TILE)
        cross = lax.dot_general(
            own_rows[...], rates[at, :], (((1,), (1,)), ((), ())), preferred_element_type=f32
        )
        normalizer = 0.5 * (own_power + power_row[:, at]) + epsilon
        coupling = (gain[:, at] * cross / normalizer).astype(bf16)
        acc[...] += jnp.dot(coupling, rates[at, : 2 * NF], preferred_element_type=f32)
        return carry

    lax.fori_loop(0, stations // TILE, pair_tile, 0)
    own_rows[:, : 2 * NF] = acc[...].astype(bf16)
    inverse_scale = 1.0 / math.sqrt(NF)

    def to_time(j, carry):
        at = pl.ds(pl.multiple_of(j * TILE, TILE), TILE)
        out[:, at] = (
            lax.dot_general(
                own_rows[:, : 2 * NF], basis[at, :], (((1,), (1,)), ((), ())),
                preferred_element_type=f32,
            )
            * inverse_scale
        ).astype(bf16)
        return carry

    lax.fori_loop(0, span // TILE, to_time, 0)

    def drain(n, carry):
        @pl.when(z < last)
        def _():
            upward(part, n).wait_send()

        @pl.when(z > 0)
        def _():
            downward(part, n).wait_send()

        to_over(n).wait_send()
        to_beside(n).wait_send()
        relay(n).wait_send()
        return carry

    lax.fori_loop(0, chunks, drain, 0)


def fused_shards(synthetic, observed, station_weights, pair_mask):
    rows, span = synthetic.shape
    stations = station_weights.shape[0]
    members = stations // rows
    chunks = rows // RC
    bf16, f32 = jnp.bfloat16, jnp.float32
    slab = pltpu.VMEM((chunks, 2 * RC, 2 * NF), bf16)
    vmem = pl.BlockSpec(memory_space=pltpu.VMEM)
    return pl.pallas_call(
        functools.partial(fused_kernel, lax.axis_size("blk"), 4.0 / math.sqrt(stations)),
        out_shape=jax.ShapeDtypeStruct((rows, span), bf16),
        in_specs=[vmem] * 4,
        out_specs=vmem,
        scratch_shapes=[
            pltpu.VMEM((span, 2 * NF), bf16),
            pltpu.VMEM((2, span // FINE, NF), f32),
            slab, slab, slab, slab, slab,
            pltpu.VMEM((members, chunks, 2 * RC, 2 * NF), bf16),
            pltpu.VMEM((rows, 4 * NF), bf16),
            pltpu.VMEM((stations, 4 * NF), bf16),
            pltpu.VMEM((stations, 128), f32),
            pltpu.VMEM((1, stations), f32),
            pltpu.VMEM((rows, stations), f32),
            pltpu.VMEM((rows, 2 * NF), f32),
            pltpu.SemaphoreType.DMA((2, chunks)),
            pltpu.SemaphoreType.DMA((2, chunks)),
            pltpu.SemaphoreType.DMA((chunks,)),
            pltpu.SemaphoreType.DMA((chunks,)),
            pltpu.SemaphoreType.DMA((chunks,)),
            pltpu.SemaphoreType.DMA((members, chunks)),
        ],
        compiler_params=pltpu.CompilerParams(
            collective_id=0, has_side_effects=True, vmem_limit_bytes=60 * 2**20
        ),
    )(synthetic, observed, station_weights.reshape(1, stations), pair_mask)


def dispatch(mesh, *arrays):
    rows, span = arrays[0].shape
    stations = arrays[2].shape[0]
    fits = 28 * NF * stations + 40 * NF * rows + 4 * rows * stations < 44 * 2**20
    whole = rows % RC == 0 and span % TILE == 0 and stations % TILE == 0
    plane = mesh.shape["sub"] == 2 and mesh.shape["pair"] == 2 and mesh.shape["blk"] > 1
    return (fused_shards if fits and whole and plane else shards)(*arrays)


def solution(mesh):
    placed = (
        P(("events", "sub", "pair"), "blk"),
        P(("events", "sub", "pair"), "blk"),
        P("events"),
        P("events", None),
    )
    return jax.shard_map(
        functools.partial(dispatch, mesh),
        mesh=mesh,
        in_specs=placed,
        out_specs=P(("events", "sub", "pair"), "blk"),
        check_vma=False,
    )
```

```python
import functools
import math

import jax
import jax.numpy as jnp
from jax import lax
from jax.experimental import pallas as pl
from jax.experimental.pallas import tpu as pltpu
from jax.sharding import PartitionSpec as P

NT = 4096
NF = 512
F_LO = 64


epsilon = 1e-06


def from_behind(value, axis, steps):
    count = lax.axis_size(axis)
    pairs = [(source, (source + steps) % count) for source in range(count)]
    return lax.ppermute(value, axis, pairs)


def make_basis(first_sample, sample_count):
    sample_index = first_sample + jnp.arange(sample_count, dtype=jnp.int32)
    bin_index = F_LO + jnp.arange(NF, dtype=jnp.int32)
    phases = sample_index[:, None] * bin_index[None, :] % NT
    angles = phases.astype(jnp.float32) * (2.0 * math.pi / NT)
    return jnp.concatenate([jnp.cos(angles), -jnp.sin(angles)], axis=1).astype(jnp.bfloat16)


def spectral_rate(spectrum):
    angular = 2.0 * math.pi / NT * (F_LO + jnp.arange(NF, dtype=jnp.int32)).astype(jnp.float32)
    widened = spectrum.astype(jnp.float32)
    return jnp.concatenate([-angular * widened[:, NF:], angular * widened[:, :NF]], axis=1).astype(
        jnp.bfloat16
    )


def shards(synthetic, observed, station_weights, pair_mask):
    cycle_size = lax.axis_size("blk")
    groups = lax.axis_size("sub") * lax.axis_size("pair")
    block_index = lax.axis_index("blk")
    member = lax.axis_index("sub") * lax.axis_size("pair") + lax.axis_index("pair")
    time_span = synthetic.shape[1]
    piece_rows = synthetic.shape[0] // cycle_size
    stations = station_weights.shape[0]
    scale_factor = 1.0 / math.sqrt(NT)
    inverse_scale = 1.0 / math.sqrt(NF)
    contract_last = (((1,), (1,)), ((), ()))
    basis_rows = make_basis(block_index * time_span, time_span)
    summed = lax.psum_scatter(
        jnp.concatenate(
            [
                jnp.dot(synthetic, basis_rows, preferred_element_type=jnp.float32),
                jnp.dot(observed, basis_rows, preferred_element_type=jnp.float32),
            ],
            axis=1,
        ).astype(jnp.bfloat16),
        "blk",
        scatter_dimension=0,
        tiled=True,
    ).astype(jnp.float32)
    model_spec = (summed[:, : 2 * NF] * scale_factor).astype(jnp.bfloat16)
    data_spec = (summed[:, 2 * NF :] * scale_factor).astype(jnp.bfloat16)
    own_rates = jnp.concatenate([spectral_rate(model_spec), spectral_rate(data_spec)], axis=1)
    block_model, block_data = (
        lax.all_gather(model_spec, ("sub", "pair"), axis=0, tiled=True),
        lax.all_gather(data_spec, ("sub", "pair"), axis=0, tiled=True),
    )
    block_power = jnp.sum(jnp.square(spectral_rate(block_model).astype(jnp.float32)), axis=1)
    gains = station_weights.astype(jnp.float32).reshape(groups * cycle_size, piece_rows)
    block_gain = lax.dynamic_slice_in_dim(
        gains.reshape(groups, cycle_size, piece_rows), block_index, 1, 1
    ).reshape(groups * piece_rows)
    link_piece = jnp.maximum(pair_mask, pair_mask.T)
    block_link = lax.dynamic_slice_in_dim(
        link_piece.reshape(groups, cycle_size, groups * cycle_size), block_index, 1, 1
    ).reshape(groups, groups * cycle_size)
    factor = 4.0 / math.sqrt(stations)

    def pair_tile(running, carried, source):
        column_model = carried[:, : 2 * NF]
        column_data = carried[:, 2 * NF :]
        column_piece = member * cycle_size + source
        column_gain = lax.dynamic_slice_in_dim(gains, column_piece, 1, 0)[0]
        column_power = jnp.sum(jnp.square(column_model.astype(jnp.float32)), axis=1)
        active_flags = lax.dynamic_slice_in_dim(block_link, column_piece, 1, 1)[:, 0]
        link_rows = jnp.broadcast_to(
            active_flags.astype(jnp.float32)[:, None], (groups, piece_rows)
        ).reshape(groups * piece_rows)
        cross_model = lax.dot_general(
            block_model, column_model, contract_last, preferred_element_type=jnp.float32
        )
        cross_data = lax.dot_general(
            block_data, column_data, contract_last, preferred_element_type=jnp.float32
        )
        normalizer = 0.5 * (block_power[:, None] + column_power[None, :]) + epsilon
        coupling = (
            factor
            * block_gain[:, None]
            * column_gain[None, :]
            * link_rows[:, None]
            * (cross_model - cross_data)
            / normalizer
        ).astype(jnp.bfloat16)
        return running + jnp.dot(coupling, column_model, preferred_element_type=jnp.float32)

    running = jnp.zeros((groups * piece_rows, 2 * NF), jnp.float32)
    running = pair_tile(running, own_rates, block_index)

    def cycle_turn(turn_index, loop_state):
        current, ahead_rates, behind_rates = loop_state
        ahead_rates = from_behind(ahead_rates, "blk", 1)
        behind_rates = from_behind(behind_rates, "blk", -1)
        current = pair_tile(current, ahead_rates, (block_index - turn_index) % cycle_size)
        current = pair_tile(current, behind_rates, (block_index + turn_index) % cycle_size)
        return (current, ahead_rates, behind_rates)

    running, ahead_rates, behind_rates = lax.fori_loop(
        1, cycle_size // 2, cycle_turn, (running, own_rates, own_rates)
    )
    ahead_rates = from_behind(ahead_rates, "blk", 1)
    running = pair_tile(running, ahead_rates, (block_index - cycle_size // 2) % cycle_size)
    adjoint_spec = lax.psum_scatter(
        running.astype(jnp.bfloat16), ("sub", "pair"), scatter_dimension=0, tiled=True
    )
    return (
        lax.dot_general(
            lax.all_gather(adjoint_spec, "blk", axis=0, tiled=True),
            basis_rows,
            contract_last,
            preferred_element_type=jnp.float32,
        )
        * inverse_scale
    ).astype(jnp.bfloat16)


MESH = pl.DeviceIdType.MESH
RC = 16
SKEW = 3
OVER = 3
BESIDE = 5
FINE = 32
TILE = 256
MEMBERS = 4
BATCH = TILE // MEMBERS


def trig(samples, shape):
    bins = F_LO + lax.broadcasted_iota(jnp.int32, shape, 1)
    angle = ((samples * bins) % NT).astype(jnp.float32) * (2.0 * math.pi / NT)
    return jnp.cos(angle), jnp.sin(angle)


def fused_kernel(
    steps_z, factor, syn, obs, weights, mask, out,
    basis, tab, part, go_up, go_down, from_low, from_high, spec, own_rows, rates,
    power_col, own_power, gain, acc,
    send_z, recv_z, send_x, send_c, send_relay, recv_g,
):
    f32, bf16 = jnp.float32, jnp.bfloat16
    event, z = lax.axis_index("events"), lax.axis_index("blk")
    sub, core = lax.axis_index("sub"), lax.axis_index("pair")
    last = steps_z - 1
    rows, span = syn.shape
    stations = weights.shape[0] * 128
    pieces = mask.shape[0]
    chunks = rows // RC
    me, across = sub * 2 + core, (1 - sub) * 2 + core
    twin, diagonal = sub * 2 + 1 - core, (1 - sub) * 2 + 1 - core
    up, down = (event, z + 1, sub, core), (event, z - 1, sub, core)
    over, beside = (event, z, 1 - sub, core), (event, z, sub, 1 - core)

    barrier = pltpu.get_barrier_semaphore()
    for device in (over, beside):
        pl.semaphore_signal(barrier, inc=1, device_id=device, device_id_type=MESH)

    @pl.when(z > 0)
    def _():
        pl.semaphore_signal(barrier, inc=1, device_id=down, device_id_type=MESH)

    @pl.when(z < last)
    def _():
        pl.semaphore_signal(barrier, inc=1, device_id=up, device_id_type=MESH)

    coarse = span // FINE
    shape = (coarse, NF)
    coarse_cos, coarse_sin = trig(
        z * span + FINE * lax.broadcasted_iota(jnp.int32, shape, 0), shape
    )
    tab[0] = coarse_cos
    tab[1] = coarse_sin
    shape = (FINE, NF)
    fine_cos, fine_sin = trig(lax.broadcasted_iota(jnp.int32, shape, 0), shape)

    def fill(a, carry):
        c = tab[0, pl.ds(a, 1), :]
        s = tab[1, pl.ds(a, 1), :]
        at = pl.ds(pl.multiple_of(a * FINE, FINE), FINE)
        basis[at, :NF] = (c * fine_cos - s * fine_sin).astype(bf16)
        basis[at, NF:] = (-(s * fine_cos + c * fine_sin)).astype(bf16)
        return carry

    lax.fori_loop(0, coarse, fill, 0)

    scale = 1.0 / math.sqrt(NT)

    def project(j, carry):
        at = pl.ds(pl.multiple_of(j * TILE, TILE), TILE)
        columns = basis[:, at]
        for k, traces in enumerate((syn, obs)):
            value = jnp.dot(traces[...], columns, preferred_element_type=f32) * scale
            part[:, k * RC : (k + 1) * RC, at] = value.astype(bf16).reshape(chunks, RC, TILE)
        return carry

    lax.fori_loop(0, 2 * NF // TILE, project, 0)

    peers = 2 + jnp.where(z > 0, 1, 0) + jnp.where(z < last, 1, 0)
    pl.semaphore_wait(barrier, peers)

    def remote(source, target, send, recv, device):
        return pltpu.make_async_remote_copy(
            src_ref=source, dst_ref=target, send_sem=send, recv_sem=recv,
            device_id=device, device_id_type=MESH,
        )

    def upward(source, n):
        return remote(source.at[n], from_low.at[n], send_z.at[0, n], recv_z.at[0, n], up)

    def downward(source, n):
        return remote(source.at[n], from_high.at[n], send_z.at[1, n], recv_z.at[1, n], down)

    def to_over(n):
        return remote(spec.at[me, n], spec.at[me, n], send_x.at[n], recv_g.at[me, n], over)

    def to_beside(n):
        return remote(spec.at[me, n], spec.at[me, n], send_c.at[n], recv_g.at[me, n], beside)

    def relay(n):
        return remote(
            spec.at[across, n], spec.at[across, n], send_relay.at[n], recv_g.at[across, n], beside
        )

    def arrived(member, n):
        remote(spec.at[member, n], spec.at[member, n], send_x.at[n], recv_g.at[member, n], over).wait_recv()

    @pl.when(z == 0)
    def _():
        lax.fori_loop(0, chunks, lambda n, c: (upward(part, n).start(), c)[1], 0)
        from_low[...] = jnp.zeros_like(from_low)

    @pl.when(z == last)
    def _():
        lax.fori_loop(0, chunks, lambda n, c: (downward(part, n).start(), c)[1], 0)
        from_high[...] = jnp.zeros_like(from_high)

    def station_of(place):
        return (place % TILE) // BATCH * rows + place // TILE * BATCH + place % BATCH

    span_piece = stations // pieces
    own_station = me * rows + lax.broadcasted_iota(jnp.int32, (rows, pieces), 0)
    behind = own_station - span_piece * lax.broadcasted_iota(jnp.int32, (rows, pieces), 1)
    own_piece = jnp.where((behind >= 0) & (behind < span_piece), 1.0, 0.0).astype(bf16)
    links = mask[...].astype(f32).astype(bf16)
    link_there = jnp.dot(own_piece, links, preferred_element_type=f32).astype(bf16)
    link_back = lax.dot_general(
        own_piece, links, (((1,), (1,)), ((), ())), preferred_element_type=f32
    ).astype(bf16)
    station = station_of(lax.broadcasted_iota(jnp.int32, (pieces, stations), 1))
    behind = station - span_piece * lax.broadcasted_iota(jnp.int32, (pieces, stations), 0)
    every_piece = jnp.where((behind >= 0) & (behind < span_piece), 1.0, 0.0).astype(bf16)
    starts = [m * rows + b * BATCH for b in range(rows // BATCH) for m in range(MEMBERS)]
    gain_row = jnp.concatenate(
        [
            weights[t // 128 : t // 128 + 1, t % 128 : t % 128 + BATCH].astype(f32)
            for t in starts
        ],
        axis=1,
    )
    column = station_of(lax.broadcasted_iota(jnp.int32, (rows, stations), 1))
    row = me * rows + lax.broadcasted_iota(jnp.int32, (rows, stations), 0)
    gain_col = jnp.sum(jnp.where(column == row, gain_row, 0.0), axis=1, keepdims=True)
    gain[...] = (factor * gain_col) * gain_row * jnp.maximum(
        jnp.dot(link_there, every_piece, preferred_element_type=f32),
        jnp.dot(link_back, every_piece, preferred_element_type=f32),
    )

    angular = 2.0 * math.pi / NT * (
        F_LO + lax.broadcasted_iota(jnp.int32, (1, NF), 1)
    ).astype(f32)

    def place_of(member, n):
        return n * RC // BATCH * TILE + member * BATCH + n * RC % BATCH

    def take(member, n):
        at = pl.ds(pl.multiple_of(place_of(member, n), RC), RC)
        value = spec[member, n].astype(f32)
        model_lo = (-angular * value[:RC, NF:]).astype(bf16)
        model_hi = (angular * value[:RC, :NF]).astype(bf16)
        rates[at, :NF] = model_lo
        rates[at, NF : 2 * NF] = model_hi
        rates[at, 2 * NF : 3 * NF] = (angular * value[RC:, NF:]).astype(bf16)
        rates[at, 3 * NF :] = (-angular * value[RC:, :NF]).astype(bf16)
        square = jnp.square(model_lo.astype(f32)) + jnp.square(model_hi.astype(f32))
        power_col[at, :] = jnp.broadcast_to(
            jnp.sum(square, axis=1, keepdims=True), (RC, 128)
        )

    eye = lax.broadcasted_iota(jnp.int32, (128, 128), 0) == lax.broadcasted_iota(
        jnp.int32, (128, 128), 1
    )

    def pair_tile(q):
        at = pl.ds(pl.multiple_of(q * TILE, TILE), TILE)
        power_row = jnp.concatenate(
            [
                jnp.sum(
                    jnp.where(
                        eye, power_col[pl.ds(pl.multiple_of(q * TILE + k, 128), 128), :], 0.0
                    ),
                    axis=0,
                    keepdims=True,
                )
                for k in range(0, TILE, 128)
            ],
            axis=1,
        )
        cross = lax.dot_general(
            own_rows[...], rates[at, :], (((1,), (1,)), ((), ())), preferred_element_type=f32
        )
        normalizer = 0.5 * (own_power[:, :1] + power_row) + epsilon
        coupling = (gain[:, at] * cross / normalizer).astype(bf16)
        acc[...] += jnp.dot(coupling, rates[at, : 2 * NF], preferred_element_type=f32)

    def within(n):
        return (n >= 0) & (n < chunks)

    acc[...] = jnp.zeros_like(acc)
    far = jnp.maximum(z, last - z)

    tiles = stations // TILE
    first_tile = max(
        [chunks] + [(q + 1) * (BATCH // RC) - 1 + BESIDE - q for q in range(tiles - 1)]
    )

    def step(s, carry):
        n_low, n_high, n_own = s - SKEW * z, s - SKEW * (last - z), s - SKEW * far

        @pl.when(within(n_low) & (z > 0))
        def _():
            upward(part, n_low).wait_recv()

            @pl.when(z < last)
            def _():
                go_up[n_low] = (part[n_low].astype(f32) + from_low[n_low].astype(f32)).astype(bf16)
                upward(go_up, n_low).start()

        @pl.when(within(n_high) & (z < last))
        def _():
            downward(part, n_high).wait_recv()

            @pl.when(z > 0)
            def _():
                go_down[n_high] = (
                    part[n_high].astype(f32) + from_high[n_high].astype(f32)
                ).astype(bf16)
                downward(go_down, n_high).start()

        @pl.when(within(n_own))
        def _():
            spec[me, n_own] = (
                part[n_own].astype(f32)
                + from_low[n_own].astype(f32)
                + from_high[n_own].astype(f32)
            ).astype(bf16)
            to_over(n_own).start()
            to_beside(n_own).start()
            at = pl.ds(pl.multiple_of(n_own * RC, RC), RC)
            own_rows[at, : 2 * NF] = spec[me, n_own, :RC, :]
            own_rows[at, 2 * NF :] = spec[me, n_own, RC:, :]
            take(me, n_own)
            own_power[at, :] = power_col[pl.ds(pl.multiple_of(place_of(me, n_own), RC), RC), :]

        @pl.when(within(n_own - OVER))
        def _():
            n = n_own - OVER
            arrived(across, n)
            relay(n).start()
            arrived(twin, n)
            take(across, n)
            take(twin, n)

        @pl.when(within(n_own - BESIDE))
        def _():
            n = n_own - BESIDE
            arrived(diagonal, n)
            take(diagonal, n)

        @pl.when((n_own >= first_tile) & (n_own < first_tile + tiles - 1))
        def _():
            pair_tile(n_own - first_tile)

        return carry

    lax.fori_loop(0, max(chunks + BESIDE, first_tile + tiles - 1) + SKEW * last, step, 0)

    pair_tile(stations // TILE - 1)
    own_rows[:, : 2 * NF] = acc[...].astype(bf16)
    inverse_scale = 1.0 / math.sqrt(NF)

    def to_time(j, carry):
        at = pl.ds(pl.multiple_of(j * TILE, TILE), TILE)
        out[:, at] = (
            lax.dot_general(
                own_rows[:, : 2 * NF], basis[at, :], (((1,), (1,)), ((), ())),
                preferred_element_type=f32,
            )
            * inverse_scale
        ).astype(bf16)
        return carry

    lax.fori_loop(0, span // TILE, to_time, 0)

    def drain(n, carry):
        @pl.when(z < last)
        def _():
            upward(part, n).wait_send()

        @pl.when(z > 0)
        def _():
            downward(part, n).wait_send()

        to_over(n).wait_send()
        to_beside(n).wait_send()
        relay(n).wait_send()
        return carry

    lax.fori_loop(0, chunks, drain, 0)


def fused_shards(synthetic, observed, station_weights, pair_mask):
    rows, span = synthetic.shape
    stations = station_weights.shape[0]
    members = stations // rows
    chunks = rows // RC
    bf16, f32 = jnp.bfloat16, jnp.float32
    weights = station_weights.reshape(stations // 128, 128)
    slab = pltpu.VMEM((chunks, 2 * RC, 2 * NF), bf16)
    vmem = pl.BlockSpec(memory_space=pltpu.VMEM)
    return pl.pallas_call(
        functools.partial(fused_kernel, lax.axis_size("blk"), 4.0 / math.sqrt(stations)),
        out_shape=jax.ShapeDtypeStruct((rows, span), bf16),
        in_specs=[vmem] * 4,
        out_specs=vmem,
        scratch_shapes=[
            pltpu.VMEM((span, 2 * NF), bf16),
            pltpu.VMEM((2, span // FINE, NF), f32),
            slab, slab, slab, slab, slab,
            pltpu.VMEM((members, chunks, 2 * RC, 2 * NF), bf16),
            pltpu.VMEM((rows, 4 * NF), bf16),
            pltpu.VMEM((stations, 4 * NF), bf16),
            pltpu.VMEM((stations, 128), f32),
            pltpu.VMEM((rows, 128), f32),
            pltpu.VMEM((rows, stations), f32),
            pltpu.VMEM((rows, 2 * NF), f32),
            pltpu.SemaphoreType.DMA((2, chunks)),
            pltpu.SemaphoreType.DMA((2, chunks)),
            pltpu.SemaphoreType.DMA((chunks,)),
            pltpu.SemaphoreType.DMA((chunks,)),
            pltpu.SemaphoreType.DMA((chunks,)),
            pltpu.SemaphoreType.DMA((members, chunks)),
        ],
        compiler_params=pltpu.CompilerParams(
            collective_id=0, has_side_effects=True, vmem_limit_bytes=40 * 2**20
        ),
    )(synthetic, observed, weights, pair_mask)


def dispatch(mesh, *arrays):
    rows, span = arrays[0].shape
    stations = arrays[2].shape[0]
    fits = 28 * NF * stations + 40 * NF * rows + 4 * rows * stations < 44 * 2**20
    whole = rows % BATCH == 0 and span % TILE == 0 and stations % TILE == 0
    plane = mesh.shape["sub"] == 2 and mesh.shape["pair"] == 2 and mesh.shape["blk"] > 1
    return (fused_shards if fits and whole and plane else shards)(*arrays)


def solution(mesh):
    placed = (
        P(("events", "sub", "pair"), "blk"),
        P(("events", "sub", "pair"), "blk"),
        P("events"),
        P("events", None),
    )
    return jax.shard_map(
        functools.partial(dispatch, mesh),
        mesh=mesh,
        in_specs=placed,
        out_specs=P(("events", "sub", "pair"), "blk"),
        check_vma=False,
    )
```

```python
import functools
import math

import jax
import jax.numpy as jnp
from jax import lax
from jax.experimental import pallas as pl
from jax.experimental.pallas import tpu as pltpu
from jax.sharding import PartitionSpec as P

NT = 4096
NF = 512
F_LO = 64


epsilon = 1e-06


def from_behind(value, axis, steps):
    count = lax.axis_size(axis)
    pairs = [(source, (source + steps) % count) for source in range(count)]
    return lax.ppermute(value, axis, pairs)


def make_basis(first_sample, sample_count):
    sample_index = first_sample + jnp.arange(sample_count, dtype=jnp.int32)
    bin_index = F_LO + jnp.arange(NF, dtype=jnp.int32)
    phases = sample_index[:, None] * bin_index[None, :] % NT
    angles = phases.astype(jnp.float32) * (2.0 * math.pi / NT)
    return jnp.concatenate([jnp.cos(angles), -jnp.sin(angles)], axis=1).astype(jnp.bfloat16)


def spectral_rate(spectrum):
    angular = 2.0 * math.pi / NT * (F_LO + jnp.arange(NF, dtype=jnp.int32)).astype(jnp.float32)
    widened = spectrum.astype(jnp.float32)
    return jnp.concatenate([-angular * widened[:, NF:], angular * widened[:, :NF]], axis=1).astype(
        jnp.bfloat16
    )


def shards(synthetic, observed, station_weights, pair_mask):
    cycle_size = lax.axis_size("blk")
    groups = lax.axis_size("sub") * lax.axis_size("pair")
    block_index = lax.axis_index("blk")
    member = lax.axis_index("sub") * lax.axis_size("pair") + lax.axis_index("pair")
    time_span = synthetic.shape[1]
    piece_rows = synthetic.shape[0] // cycle_size
    stations = station_weights.shape[0]
    scale_factor = 1.0 / math.sqrt(NT)
    inverse_scale = 1.0 / math.sqrt(NF)
    contract_last = (((1,), (1,)), ((), ()))
    basis_rows = make_basis(block_index * time_span, time_span)
    summed = lax.psum_scatter(
        jnp.concatenate(
            [
                jnp.dot(synthetic, basis_rows, preferred_element_type=jnp.float32),
                jnp.dot(observed, basis_rows, preferred_element_type=jnp.float32),
            ],
            axis=1,
        ).astype(jnp.bfloat16),
        "blk",
        scatter_dimension=0,
        tiled=True,
    ).astype(jnp.float32)
    model_spec = (summed[:, : 2 * NF] * scale_factor).astype(jnp.bfloat16)
    data_spec = (summed[:, 2 * NF :] * scale_factor).astype(jnp.bfloat16)
    own_rates = jnp.concatenate([spectral_rate(model_spec), spectral_rate(data_spec)], axis=1)
    block_model, block_data = (
        lax.all_gather(model_spec, ("sub", "pair"), axis=0, tiled=True),
        lax.all_gather(data_spec, ("sub", "pair"), axis=0, tiled=True),
    )
    block_power = jnp.sum(jnp.square(spectral_rate(block_model).astype(jnp.float32)), axis=1)
    gains = station_weights.astype(jnp.float32).reshape(groups * cycle_size, piece_rows)
    block_gain = lax.dynamic_slice_in_dim(
        gains.reshape(groups, cycle_size, piece_rows), block_index, 1, 1
    ).reshape(groups * piece_rows)
    link_piece = jnp.maximum(pair_mask, pair_mask.T)
    block_link = lax.dynamic_slice_in_dim(
        link_piece.reshape(groups, cycle_size, groups * cycle_size), block_index, 1, 1
    ).reshape(groups, groups * cycle_size)
    factor = 4.0 / math.sqrt(stations)

    def pair_tile(running, carried, source):
        column_model = carried[:, : 2 * NF]
        column_data = carried[:, 2 * NF :]
        column_piece = member * cycle_size + source
        column_gain = lax.dynamic_slice_in_dim(gains, column_piece, 1, 0)[0]
        column_power = jnp.sum(jnp.square(column_model.astype(jnp.float32)), axis=1)
        active_flags = lax.dynamic_slice_in_dim(block_link, column_piece, 1, 1)[:, 0]
        link_rows = jnp.broadcast_to(
            active_flags.astype(jnp.float32)[:, None], (groups, piece_rows)
        ).reshape(groups * piece_rows)
        cross_model = lax.dot_general(
            block_model, column_model, contract_last, preferred_element_type=jnp.float32
        )
        cross_data = lax.dot_general(
            block_data, column_data, contract_last, preferred_element_type=jnp.float32
        )
        normalizer = 0.5 * (block_power[:, None] + column_power[None, :]) + epsilon
        coupling = (
            factor
            * block_gain[:, None]
            * column_gain[None, :]
            * link_rows[:, None]
            * (cross_model - cross_data)
            / normalizer
        ).astype(jnp.bfloat16)
        return running + jnp.dot(coupling, column_model, preferred_element_type=jnp.float32)

    running = jnp.zeros((groups * piece_rows, 2 * NF), jnp.float32)
    running = pair_tile(running, own_rates, block_index)

    def cycle_turn(turn_index, loop_state):
        current, ahead_rates, behind_rates = loop_state
        ahead_rates = from_behind(ahead_rates, "blk", 1)
        behind_rates = from_behind(behind_rates, "blk", -1)
        current = pair_tile(current, ahead_rates, (block_index - turn_index) % cycle_size)
        current = pair_tile(current, behind_rates, (block_index + turn_index) % cycle_size)
        return (current, ahead_rates, behind_rates)

    running, ahead_rates, behind_rates = lax.fori_loop(
        1, cycle_size // 2, cycle_turn, (running, own_rates, own_rates)
    )
    ahead_rates = from_behind(ahead_rates, "blk", 1)
    running = pair_tile(running, ahead_rates, (block_index - cycle_size // 2) % cycle_size)
    adjoint_spec = lax.psum_scatter(
        running.astype(jnp.bfloat16), ("sub", "pair"), scatter_dimension=0, tiled=True
    )
    return (
        lax.dot_general(
            lax.all_gather(adjoint_spec, "blk", axis=0, tiled=True),
            basis_rows,
            contract_last,
            preferred_element_type=jnp.float32,
        )
        * inverse_scale
    ).astype(jnp.bfloat16)


MESH = pl.DeviceIdType.MESH
RC = 16
SKEW = 3
OVER = 3
BESIDE = 5
FINE = 32
TILE = 256
MEMBERS = 4
BATCH = TILE // MEMBERS


def trig(samples, shape):
    bins = F_LO + lax.broadcasted_iota(jnp.int32, shape, 1)
    angle = ((samples * bins) % NT).astype(jnp.float32) * (2.0 * math.pi / NT)
    return jnp.cos(angle), jnp.sin(angle)


def fused_kernel(
    steps_z, factor, syn_hbm, obs_hbm, weights_hbm, mask_hbm, out,
    syn, obs, weights, mask,
    basis, tab, part, go_up, go_down, from_low, from_high, spec, own_rows, rates,
    power_col, own_power, gain, acc,
    send_z, recv_z, send_x, send_c, send_relay, recv_g, load,
):
    f32, bf16 = jnp.float32, jnp.bfloat16
    event, z = lax.axis_index("events"), lax.axis_index("blk")
    sub, core = lax.axis_index("sub"), lax.axis_index("pair")
    last = steps_z - 1
    rows, span = syn.shape
    stations = weights.shape[0] * 128
    pieces = mask.shape[0]
    chunks = rows // RC
    me, across = sub * 2 + core, (1 - sub) * 2 + core
    twin, diagonal = sub * 2 + 1 - core, (1 - sub) * 2 + 1 - core
    up, down = (event, z + 1, sub, core), (event, z - 1, sub, core)
    over, beside = (event, z, 1 - sub, core), (event, z, sub, 1 - core)

    loads = [
        pltpu.make_async_copy(source, target, load.at[k])
        for k, (source, target) in enumerate(
            ((syn_hbm, syn), (obs_hbm, obs), (weights_hbm, weights), (mask_hbm, mask))
        )
    ]
    for copy in loads:
        copy.start()

    barrier = pltpu.get_barrier_semaphore()
    for device in (over, beside):
        pl.semaphore_signal(barrier, inc=1, device_id=device, device_id_type=MESH)

    @pl.when(z > 0)
    def _():
        pl.semaphore_signal(barrier, inc=1, device_id=down, device_id_type=MESH)

    @pl.when(z < last)
    def _():
        pl.semaphore_signal(barrier, inc=1, device_id=up, device_id_type=MESH)

    coarse = span // FINE
    shape = (coarse, NF)
    coarse_cos, coarse_sin = trig(
        z * span + FINE * lax.broadcasted_iota(jnp.int32, shape, 0), shape
    )
    tab[0] = coarse_cos
    tab[1] = coarse_sin
    shape = (FINE, NF)
    fine_cos, fine_sin = trig(lax.broadcasted_iota(jnp.int32, shape, 0), shape)

    def fill(a, carry):
        c = tab[0, pl.ds(a, 1), :]
        s = tab[1, pl.ds(a, 1), :]
        at = pl.ds(pl.multiple_of(a * FINE, FINE), FINE)
        basis[at, :NF] = (c * fine_cos - s * fine_sin).astype(bf16)
        basis[at, NF:] = (-(s * fine_cos + c * fine_sin)).astype(bf16)
        return carry

    lax.fori_loop(0, coarse, fill, 0)

    scale = 1.0 / math.sqrt(NT)

    def project(first, count):
        def columns_of(j, carry):
            at = pl.ds(pl.multiple_of(j * TILE, TILE), TILE)
            columns = basis[:, at]
            for k, traces in enumerate((syn, obs)):
                value = scale * jnp.dot(
                    traces[first * RC : (first + count) * RC, :],
                    columns,
                    preferred_element_type=f32,
                )
                part[first : first + count, k * RC : (k + 1) * RC, at] = value.astype(
                    bf16
                ).reshape(count, RC, TILE)
            return carry

        lax.fori_loop(0, 2 * NF // TILE, columns_of, 0)

    for copy in loads[:2]:
        copy.wait()
    early = BATCH // RC
    project(0, early)

    peers = 2 + jnp.where(z > 0, 1, 0) + jnp.where(z < last, 1, 0)
    pl.semaphore_wait(barrier, peers)

    def remote(source, target, send, recv, device):
        return pltpu.make_async_remote_copy(
            src_ref=source, dst_ref=target, send_sem=send, recv_sem=recv,
            device_id=device, device_id_type=MESH,
        )

    def upward(source, n):
        return remote(source.at[n], from_low.at[n], send_z.at[0, n], recv_z.at[0, n], up)

    def downward(source, n):
        return remote(source.at[n], from_high.at[n], send_z.at[1, n], recv_z.at[1, n], down)

    def to_over(n):
        return remote(spec.at[me, n], spec.at[me, n], send_x.at[n], recv_g.at[me, n], over)

    def to_beside(n):
        return remote(spec.at[me, n], spec.at[me, n], send_c.at[n], recv_g.at[me, n], beside)

    def relay(n):
        return remote(
            spec.at[across, n], spec.at[across, n], send_relay.at[n], recv_g.at[across, n], beside
        )

    def arrived(member, n):
        remote(spec.at[member, n], spec.at[member, n], send_x.at[n], recv_g.at[member, n], over).wait_recv()

    def launch(first, end):
        @pl.when(z == 0)
        def _():
            lax.fori_loop(first, end, lambda n, c: (upward(part, n).start(), c)[1], 0)

        @pl.when(z == last)
        def _():
            lax.fori_loop(first, end, lambda n, c: (downward(part, n).start(), c)[1], 0)

    launch(0, early)
    project(early, chunks - early)
    launch(early, chunks)

    @pl.when(z == 0)
    def _():
        from_low[...] = jnp.zeros_like(from_low)

    @pl.when(z == last)
    def _():
        from_high[...] = jnp.zeros_like(from_high)

    for copy in loads[2:]:
        copy.wait()

    def station_of(place):
        return (place % TILE) // BATCH * rows + place // TILE * BATCH + place % BATCH

    span_piece = stations // pieces
    own_station = me * rows + lax.broadcasted_iota(jnp.int32, (rows, pieces), 0)
    behind = own_station - span_piece * lax.broadcasted_iota(jnp.int32, (rows, pieces), 1)
    own_piece = jnp.where((behind >= 0) & (behind < span_piece), 1.0, 0.0).astype(bf16)
    links = mask[...].astype(f32).astype(bf16)
    link_there = jnp.dot(own_piece, links, preferred_element_type=f32).astype(bf16)
    link_back = lax.dot_general(
        own_piece, links, (((1,), (1,)), ((), ())), preferred_element_type=f32
    ).astype(bf16)
    station = station_of(lax.broadcasted_iota(jnp.int32, (pieces, stations), 1))
    behind = station - span_piece * lax.broadcasted_iota(jnp.int32, (pieces, stations), 0)
    every_piece = jnp.where((behind >= 0) & (behind < span_piece), 1.0, 0.0).astype(bf16)
    starts = [m * rows + b * BATCH for b in range(rows // BATCH) for m in range(MEMBERS)]
    gain_row = jnp.concatenate(
        [
            weights[t // 128 : t // 128 + 1, t % 128 : t % 128 + BATCH].astype(f32)
            for t in starts
        ],
        axis=1,
    )
    column = station_of(lax.broadcasted_iota(jnp.int32, (rows, stations), 1))
    row = me * rows + lax.broadcasted_iota(jnp.int32, (rows, stations), 0)
    gain_col = jnp.sum(jnp.where(column == row, gain_row, 0.0), axis=1, keepdims=True)
    gain[...] = (factor * gain_col) * gain_row * jnp.maximum(
        jnp.dot(link_there, every_piece, preferred_element_type=f32),
        jnp.dot(link_back, every_piece, preferred_element_type=f32),
    )

    angular = 2.0 * math.pi / NT * (
        F_LO + lax.broadcasted_iota(jnp.int32, (1, NF), 1)
    ).astype(f32)

    def place_of(member, n):
        return n * RC // BATCH * TILE + member * BATCH + n * RC % BATCH

    def take(member, n):
        at = pl.ds(pl.multiple_of(place_of(member, n), RC), RC)
        value = spec[member, n].astype(f32)
        model_lo = (-angular * value[:RC, NF:]).astype(bf16)
        model_hi = (angular * value[:RC, :NF]).astype(bf16)
        rates[at, :NF] = model_lo
        rates[at, NF : 2 * NF] = model_hi
        rates[at, 2 * NF : 3 * NF] = (angular * value[RC:, NF:]).astype(bf16)
        rates[at, 3 * NF :] = (-angular * value[RC:, :NF]).astype(bf16)
        square = jnp.square(model_lo.astype(f32)) + jnp.square(model_hi.astype(f32))
        power_col[at, :] = jnp.broadcast_to(
            jnp.sum(square, axis=1, keepdims=True), (RC, 128)
        )

    eye = lax.broadcasted_iota(jnp.int32, (128, 128), 0) == lax.broadcasted_iota(
        jnp.int32, (128, 128), 1
    )

    def pair_tile(q):
        at = pl.ds(pl.multiple_of(q * TILE, TILE), TILE)
        power_row = jnp.concatenate(
            [
                jnp.sum(
                    jnp.where(
                        eye, power_col[pl.ds(pl.multiple_of(q * TILE + k, 128), 128), :], 0.0
                    ),
                    axis=0,
                    keepdims=True,
                )
                for k in range(0, TILE, 128)
            ],
            axis=1,
        )
        cross = lax.dot_general(
            own_rows[...], rates[at, :], (((1,), (1,)), ((), ())), preferred_element_type=f32
        )
        normalizer = 0.5 * (own_power[:, :1] + power_row) + epsilon
        coupling = (gain[:, at] * cross / normalizer).astype(bf16)
        acc[...] += jnp.dot(coupling, rates[at, : 2 * NF], preferred_element_type=f32)

    def within(n):
        return (n >= 0) & (n < chunks)

    acc[...] = jnp.zeros_like(acc)
    far = jnp.maximum(z, last - z)

    tiles = stations // TILE
    first_tile = max(
        [chunks] + [(q + 1) * (BATCH // RC) - 1 + BESIDE - q for q in range(tiles - 1)]
    )

    def step(s, carry):
        n_low, n_high, n_own = s - SKEW * z, s - SKEW * (last - z), s - SKEW * far

        @pl.when(within(n_low) & (z > 0))
        def _():
            upward(part, n_low).wait_recv()

            @pl.when(z < last)
            def _():
                go_up[n_low] = (part[n_low].astype(f32) + from_low[n_low].astype(f32)).astype(bf16)
                upward(go_up, n_low).start()

        @pl.when(within(n_high) & (z < last))
        def _():
            downward(part, n_high).wait_recv()

            @pl.when(z > 0)
            def _():
                go_down[n_high] = (
                    part[n_high].astype(f32) + from_high[n_high].astype(f32)
                ).astype(bf16)
                downward(go_down, n_high).start()

        @pl.when(within(n_own))
        def _():
            spec[me, n_own] = (
                part[n_own].astype(f32)
                + from_low[n_own].astype(f32)
                + from_high[n_own].astype(f32)
            ).astype(bf16)
            to_over(n_own).start()
            to_beside(n_own).start()
            at = pl.ds(pl.multiple_of(n_own * RC, RC), RC)
            own_rows[at, : 2 * NF] = spec[me, n_own, :RC, :]
            own_rows[at, 2 * NF :] = spec[me, n_own, RC:, :]
            take(me, n_own)
            own_power[at, :] = power_col[pl.ds(pl.multiple_of(place_of(me, n_own), RC), RC), :]

        @pl.when(within(n_own - OVER))
        def _():
            n = n_own - OVER
            arrived(across, n)
            relay(n).start()
            arrived(twin, n)
            take(across, n)
            take(twin, n)

        @pl.when(within(n_own - BESIDE))
        def _():
            n = n_own - BESIDE
            arrived(diagonal, n)
            take(diagonal, n)

        @pl.when((n_own >= first_tile) & (n_own < first_tile + tiles - 1))
        def _():
            pair_tile(n_own - first_tile)

        return carry

    lax.fori_loop(0, max(chunks + BESIDE, first_tile + tiles - 1) + SKEW * last, step, 0)

    pair_tile(stations // TILE - 1)
    own_rows[:, : 2 * NF] = acc[...].astype(bf16)
    inverse_scale = 1.0 / math.sqrt(NF)

    def to_time(j, carry):
        at = pl.ds(pl.multiple_of(j * TILE, TILE), TILE)
        out[:, at] = (
            lax.dot_general(
                own_rows[:, : 2 * NF], basis[at, :], (((1,), (1,)), ((), ())),
                preferred_element_type=f32,
            )
            * inverse_scale
        ).astype(bf16)
        return carry

    lax.fori_loop(0, span // TILE, to_time, 0)

    def drain(n, carry):
        @pl.when(z < last)
        def _():
            upward(part, n).wait_send()

        @pl.when(z > 0)
        def _():
            downward(part, n).wait_send()

        to_over(n).wait_send()
        to_beside(n).wait_send()
        relay(n).wait_send()
        return carry

    lax.fori_loop(0, chunks, drain, 0)


def fused_shards(synthetic, observed, station_weights, pair_mask):
    rows, span = synthetic.shape
    stations = station_weights.shape[0]
    members = stations // rows
    chunks = rows // RC
    bf16, f32 = jnp.bfloat16, jnp.float32
    weights = station_weights.reshape(stations // 128, 128)
    slab = pltpu.VMEM((chunks, 2 * RC, 2 * NF), bf16)
    vmem = pl.BlockSpec(memory_space=pltpu.VMEM)
    return pl.pallas_call(
        functools.partial(fused_kernel, lax.axis_size("blk"), 4.0 / math.sqrt(stations)),
        out_shape=jax.ShapeDtypeStruct((rows, span), bf16),
        in_specs=[pl.BlockSpec(memory_space=pltpu.HBM)] * 4,
        out_specs=vmem,
        scratch_shapes=[
            pltpu.VMEM((rows, span), bf16),
            pltpu.VMEM((rows, span), bf16),
            pltpu.VMEM((stations // 128, 128), jnp.int32),
            pltpu.VMEM(pair_mask.shape, jnp.int32),
            pltpu.VMEM((span, 2 * NF), bf16),
            pltpu.VMEM((2, span // FINE, NF), f32),
            slab, slab, slab, slab, slab,
            pltpu.VMEM((members, chunks, 2 * RC, 2 * NF), bf16),
            pltpu.VMEM((rows, 4 * NF), bf16),
            pltpu.VMEM((stations, 4 * NF), bf16),
            pltpu.VMEM((stations, 128), f32),
            pltpu.VMEM((rows, 128), f32),
            pltpu.VMEM((rows, stations), f32),
            pltpu.VMEM((rows, 2 * NF), f32),
            pltpu.SemaphoreType.DMA((2, chunks)),
            pltpu.SemaphoreType.DMA((2, chunks)),
            pltpu.SemaphoreType.DMA((chunks,)),
            pltpu.SemaphoreType.DMA((chunks,)),
            pltpu.SemaphoreType.DMA((chunks,)),
            pltpu.SemaphoreType.DMA((members, chunks)),
            pltpu.SemaphoreType.DMA((4,)),
        ],
        compiler_params=pltpu.CompilerParams(
            collective_id=0, has_side_effects=True, vmem_limit_bytes=60 * 2**20
        ),
    )(synthetic, observed, weights, pair_mask)


def dispatch(mesh, *arrays):
    rows, span = arrays[0].shape
    stations = arrays[2].shape[0]
    fits = 28 * NF * stations + 40 * NF * rows + 4 * rows * stations < 44 * 2**20
    whole = rows % BATCH == 0 and span % TILE == 0 and stations % TILE == 0
    plane = mesh.shape["sub"] == 2 and mesh.shape["pair"] == 2 and mesh.shape["blk"] > 1
    return (fused_shards if fits and whole and plane else shards)(*arrays)


def solution(mesh):
    placed = (
        P(("events", "sub", "pair"), "blk"),
        P(("events", "sub", "pair"), "blk"),
        P("events"),
        P("events", None),
    )
    return jax.shard_map(
        functools.partial(dispatch, mesh),
        mesh=mesh,
        in_specs=placed,
        out_specs=P(("events", "sub", "pair"), "blk"),
        check_vma=False,
    )
```
